32 devices in a mesh: dp: 4 (over y, core), ctx: 4 (over z), tsp: 2 (over x).
Axes of the slice: x: 2, y: 2, z: 4, core: 2. Of those that a mesh axis runs over, the one named last changes fastest.
Arguments:
- grad_out: bfloat16 [4, 1024, 8192], P('dp', 'ctx', 'tsp'), may hold values from -6 to 6
- attn_out: bfloat16 [4, 1024, 4096], P('dp', None, 'ctx'), may hold values from -6 to 6
- out_weight: bfloat16 [4096, 8192], P('ctx', 'tsp'), may hold values from -0.0625 to 0.0625
- query: bfloat16 [4, 1024, 4096], P('dp', 'tsp', 'ctx'), may hold values from -128 to 128
- keys: bfloat16 [4, 1024, 512], P('dp'), may hold values from -128 to 128
- values: bfloat16 [4, 1024, 512], P('dp'), may hold values from -6 to 6
- segment_ids: int32 [4, 1024], P('dp'), may hold values from 0 to 7, never falling along the last dimension, each value on 1 to 256 neighbouring positions
- tile_live: int32 [4, 8, 8], P('dp'), may hold values 0 or 1
Outputs:
- grad_query: bfloat16 [4, 1024, 4096], P('dp', 'tsp', 'ctx')
- grad_keys: bfloat16 [4, 1024, 512], P('dp', ('ctx', 'tsp'))
- grad_values: bfloat16 [4, 1024, 512], P('dp', ('ctx', 'tsp'))
- grad_weight: float32 [4096, 8192], P('ctx', 'tsp')
The draws below stay inside these ranges and needn't reach their ends.
Inputs may be any that keep to these rules, and one draw needn't show every extreme that they name: `segment_ids`: segment numbers never fall along a row and segment 0 is the source document; each segment has 1 to 256 tokens, one exactly that many.
All inputs are finite; a program needn't handle non-finite values. No bound on the sum of `tile_live` on one device may be relied on, other than what follows from the above.
Results may differ from the reference program's by a relative error of at most 0.0058.
Values may be sent and summed in bfloat16 or wider, within the bound.
A program may use at most 128 MiB of HBM per device.

```python
import math
import jax
import jax.numpy as jnp
import numpy as np
from jax import lax

D = 8192
HEADS = 32
KV_HEADS = 4
HEAD_DIM = 128
TILE = 128
SEGS = 8
SEQ = 1024
BATCH = 4


def shared_pair(key):
    base = jax.random.fold_in(key, 4242)
    key_vals = jax.random.normal(jax.random.fold_in(base, 1), (BATCH, SEQ, KV_HEADS * HEAD_DIM), jnp.float32)
    query_vals = jax.random.normal(jax.random.fold_in(base, 2), (BATCH, SEQ, HEADS * HEAD_DIM), jnp.float32)
    return (query_vals, key_vals)


def draw_query(key, part):
    return shared_pair(key)[0].astype(jnp.bfloat16)


def draw_keys(key, part):
    return shared_pair(key)[1].astype(jnp.bfloat16)


def with_ends(values, own_key, least, largest):
    extent = values.shape
    index_at = [jax.random.randint(jax.random.fold_in(own_key, axis), (), 0, extent[axis]) for axis in range(len(extent))]
    values = values.at[tuple(index_at)].set(least)
    longest = extent.index(max(extent))
    index_at[longest] = (index_at[longest] + 1) % extent[longest]
    return values.at[tuple(index_at)].set(largest)


def steps_of(stream_key, extent, cuts, smallest, top_value):
    level = 1.0
    for dim, blocks in cuts:
        draws = jax.random.uniform(jax.random.fold_in(jax.random.fold_in(stream_key, 6), dim), (blocks,), jnp.float32, smallest / len(cuts), top_value / len(cuts))
        level = level * jnp.repeat(jnp.exp(draws), extent[dim] // blocks).reshape((-1,) + (1,) * (len(extent) - 1 - dim))
    return level


def profile(number_of, total, limit, lean):
    portions = [(1 << 20) // math.isqrt(grade ** lean) + 1 for grade in range(2, number_of + 1)]
    rest, given = total - limit - (number_of - 1), [1] * (number_of - 1)
    while rest > 0:
        movable = [i for i in range(number_of - 1) if given[i] < limit]
        whole, remaining = sum([portions[i] for i in movable]), rest
        for i in movable:
            more = min(limit - given[i], max(1, remaining * portions[i] // whole), rest)
            given[i] = given[i] + more
            rest = rest - more
    return np.array([limit] + given)


def ragged_sizes(own_key, number_of, total, reach, skew):
    if number_of == 2:
        one = jax.random.randint(own_key, (), max(1, total - reach), min(reach, total - 1) + 1)
        return jnp.stack([one, total - one])
    sizes = jnp.asarray(profile(number_of, total, reach, skew), jnp.int32)
    twos = (number_of - 1) // 2
    donor, taker = sizes[1:1 + 2 * twos:2], sizes[2:2 + 2 * twos:2]
    slack = jnp.minimum(donor - 1, reach - taker)
    passed = jax.random.randint(jax.random.fold_in(own_key, 1), (twos,), 0, 1 << 20) % (slack + 1)
    sizes = sizes.at[1:1 + 2 * twos:2].set(donor - passed).at[2:2 + 2 * twos:2].set(taker + passed)
    return sizes[jax.random.permutation(jax.random.fold_in(own_key, 2), number_of)]


def centred(own_key, shape, width, bound, shards=(), kind=jnp.bfloat16):
    loudness = steps_of(own_key, shape, shards, -0.22, 0.18) if shards else 1.0
    entries = jax.random.normal(own_key, shape, jnp.float32) * width * loudness
    return jnp.minimum(jnp.maximum(entries, -bound), bound).astype(kind)


def setup_inputs(seed: int = 0) -> dict:
    seeds = jax.random.split(jax.random.key(seed), 9)
    return {
        "grad_out": centred(seeds[0], (BATCH, SEQ, D), 1.0, 6.0, ((0, 4), (1, 4), (2, 2))),
        "attn_out": centred(seeds[1], (BATCH, SEQ, HEADS * HEAD_DIM), 1.0, 6.0, ((0, 4), (2, 4))),
        "out_weight": centred(seeds[2], (HEADS * HEAD_DIM, D), D ** -0.5, 0.0625, ((0, 4), (1, 2))),
        "query": draw_query(jax.random.fold_in(seeds[8], 71), 0),
        "keys": draw_keys(jax.random.fold_in(seeds[8], 71), 0),
        "values": centred(seeds[5], (BATCH, SEQ, KV_HEADS * HEAD_DIM), 1.0, 6.0, ((0, 4),)),
        "segment_ids": jax.vmap(lambda own: jnp.searchsorted(jnp.cumsum(ragged_sizes(own, SEGS, SEQ, SEQ // 4, 2)), jnp.arange(SEQ), side="right"))(jax.random.split(seeds[6], BATCH)).reshape((BATCH, SEQ)).astype(jnp.int32),
        "tile_live": with_ends((jax.random.randint(seeds[7], (BATCH, SEQ // TILE, SEQ // TILE), 0, 4) < 3).astype(jnp.int32), jax.random.fold_in(seeds[7], 1), 0, 1),
    }


def row_backward(grad_row, out_row, weight, query_row, key_row, value_row, segment_row, tile_row):
    score_scale = 1.0 / math.sqrt(HEAD_DIM)
    out_grad = jnp.dot(grad_row, weight.T, preferred_element_type=jnp.float32).astype(jnp.bfloat16)
    weight_term = jnp.dot(out_row.T, grad_row, preferred_element_type=jnp.float32)
    places = jnp.arange(SEQ, dtype=jnp.int32)
    tile_of = places // TILE
    tile_mask = (tile_row[tile_of[:, None], tile_of[None, :]] == 1) | (tile_of[:, None] == tile_of[None, :])
    same_doc = (segment_row[None, :] == segment_row[:, None]) | (segment_row[None, :] == 0)
    allowed = tile_mask & same_doc & (places[None, :] <= places[:, None])
    group_size = HEADS // KV_HEADS
    query_table = query_row.reshape(SEQ, HEADS, HEAD_DIM)
    grad_table = out_grad.reshape(SEQ, HEADS, HEAD_DIM)
    output_table = out_row.reshape(SEQ, HEADS, HEAD_DIM)
    key_table = key_row.reshape(SEQ, KV_HEADS, HEAD_DIM)
    value_table = value_row.reshape(SEQ, KV_HEADS, HEAD_DIM)

    def one_head(head_index):
        kv_index = head_index // group_size
        query_head = lax.dynamic_index_in_dim(query_table, head_index, 1, keepdims=False)
        grad_head = lax.dynamic_index_in_dim(grad_table, head_index, 1, keepdims=False)
        output_head = lax.dynamic_index_in_dim(output_table, head_index, 1, keepdims=False)
        key_head = lax.dynamic_index_in_dim(key_table, kv_index, 1, keepdims=False)
        value_head = lax.dynamic_index_in_dim(value_table, kv_index, 1, keepdims=False)
        scores = jnp.dot(query_head, key_head.T, preferred_element_type=jnp.float32) * score_scale
        scores = jnp.where(allowed, scores, -jnp.inf)
        row_max = lax.optimization_barrier(jnp.max(scores, axis=1, keepdims=True))
        lse = row_max + jnp.log(lax.optimization_barrier(jnp.sum(jnp.exp(scores - row_max), axis=1, keepdims=True)))
        probs_f = jnp.where(allowed, jnp.exp(scores - lse), 0.0)
        probs = probs_f.astype(jnp.bfloat16)
        value_term = jnp.dot(probs.T, grad_head, preferred_element_type=jnp.float32)
        dprobs = jnp.dot(grad_head, value_head.T, preferred_element_type=jnp.float32)
        delta = lax.optimization_barrier(jnp.sum(grad_head.astype(jnp.float32) * output_head.astype(jnp.float32), axis=1, keepdims=True))
        dscores = (probs_f * (dprobs - delta)).astype(jnp.bfloat16)
        query_grad = (jnp.dot(dscores, key_head, preferred_element_type=jnp.float32) * score_scale).astype(jnp.bfloat16)
        key_term = jnp.dot(dscores.T, query_head, preferred_element_type=jnp.float32) * score_scale
        return (query_grad, key_term, value_term)
    query_grads, key_terms, value_terms = lax.map(one_head, jnp.arange(HEADS, dtype=jnp.int32))
    grad_query = query_grads.transpose(1, 0, 2).reshape(SEQ, HEADS * HEAD_DIM)
    key_sum = key_terms.reshape(KV_HEADS, group_size, SEQ, HEAD_DIM).sum(axis=1)
    value_sum = value_terms.reshape(KV_HEADS, group_size, SEQ, HEAD_DIM).sum(axis=1)
    grad_keys = key_sum.transpose(1, 0, 2).reshape(SEQ, KV_HEADS * HEAD_DIM).astype(jnp.bfloat16)
    grad_values = value_sum.transpose(1, 0, 2).reshape(SEQ, KV_HEADS * HEAD_DIM).astype(jnp.bfloat16)
    return (grad_query, grad_keys, grad_values, weight_term)

def reference(grad_out, attn_out, out_weight, query, keys, values, segment_ids, tile_live):
    query_list = []
    key_list = []
    value_list = []
    weight_total = jnp.zeros((HEADS * HEAD_DIM, D), jnp.float32)
    for row_index in range(BATCH):
        parts = row_backward(grad_out[row_index], attn_out[row_index], out_weight, query[row_index], keys[row_index], values[row_index], segment_ids[row_index], tile_live[row_index])
        query_list.append(parts[0])
        key_list.append(parts[1])
        value_list.append(parts[2])
        weight_total = weight_total + parts[3]
    return (jnp.stack(query_list), jnp.stack(key_list), jnp.stack(value_list), weight_total)
```

```python
import math

import jax
import jax.numpy as jnp
from jax import lax
from jax.sharding import PartitionSpec as P

HEADS = 32
KV_HEADS = 4
HEAD_DIM = 128
TILE = 128


def merge_group(tensor_in):
    row_count = tensor_in.shape[0]
    folded = tensor_in.reshape(row_count, KV_HEADS, HEADS // KV_HEADS, HEAD_DIM).sum(axis=2)
    return folded.reshape(row_count, KV_HEADS * HEAD_DIM)


def per_device(grad_out, attn_out, out_weight, query, keys, values, segment_ids, tile_live):
    score_scale = 1.0 / math.sqrt(HEAD_DIM)
    out_all = attn_out[0]
    seq_len = out_all.shape[0]
    feat_width = out_all.shape[1]
    dy_block = lax.all_gather(grad_out, "ctx", axis=1, tiled=True)[0]
    proj_rows = lax.dot_general(
        dy_block, out_weight, (((1,), (1,)), ((), ())), preferred_element_type=jnp.float32
    )
    grad_part = proj_rows
    weight_part = lax.dot_general(
        out_all, dy_block, (((0,), (0,)), ((), ())), preferred_element_type=jnp.float32
    )
    grad_part, weight_part = (grad_part, weight_part)
    weight_quarter = lax.psum_scatter(weight_part, "dp", scatter_dimension=0, tiled=True)
    grad_weight = lax.all_gather(
        weight_quarter.astype(jnp.bfloat16), "dp", axis=0, tiled=True
    ).astype(jnp.float32)
    out_grad = lax.psum_scatter(grad_part, "tsp", scatter_dimension=0, tiled=True).astype(
        jnp.bfloat16
    )
    quarter = out_grad.shape[0]
    row_start = lax.axis_index("tsp") * quarter
    heads_dev = feat_width // HEAD_DIM
    group_size = HEADS // KV_HEADS
    head_ids = lax.axis_index("ctx") * heads_dev + jnp.arange(heads_dev, dtype=jnp.int32)
    kv_ids = head_ids // group_size
    query_pos = row_start + jnp.arange(quarter, dtype=jnp.int32)
    key_pos = jnp.arange(seq_len, dtype=jnp.int32)
    tile_count = seq_len // TILE
    tile_rows = lax.dynamic_slice_in_dim(tile_live[0], row_start // TILE, quarter // TILE, 0)
    tile_mask = (
        jnp.broadcast_to(
            tile_rows[:, None, :, None], (quarter // TILE, TILE, tile_count, TILE)
        ).reshape(quarter, seq_len)
        == 1
    )
    same_tile = query_pos[:, None] // TILE == key_pos[None, :] // TILE
    segments = segment_ids[0]
    query_seg = lax.dynamic_slice_in_dim(segments, row_start, quarter, 0)
    same_doc = (segments[None, :] == query_seg[:, None]) | (segments[None, :] == 0)
    allowed = (tile_mask | same_tile) & same_doc & (key_pos[None, :] <= query_pos[:, None])

    def split_heads(tensor_in):
        return tensor_in.reshape(tensor_in.shape[0], heads_dev, HEAD_DIM).transpose(1, 0, 2)

    query_heads = split_heads(query[0])
    grad_heads = split_heads(out_grad)
    output_heads = split_heads(lax.dynamic_slice_in_dim(out_all, row_start, quarter, 0))
    key_table = keys[0].reshape(seq_len, KV_HEADS, HEAD_DIM)
    value_table = values[0].reshape(seq_len, KV_HEADS, HEAD_DIM)

    def one_head(head_items):
        query_head, grad_head, output_head, kv_index = head_items
        key_head = lax.dynamic_index_in_dim(key_table, kv_index, 1, keepdims=False)
        value_head = lax.dynamic_index_in_dim(value_table, kv_index, 1, keepdims=False)
        scores = (
            lax.dot_general(
                query_head, key_head, (((1,), (1,)), ((), ())), preferred_element_type=jnp.float32
            )
            * score_scale
        )
        scores = jnp.where(allowed, scores, -jnp.inf)
        row_max = jnp.max(scores, axis=1, keepdims=True)
        lse = row_max + jnp.log(jnp.sum(jnp.exp(scores - row_max), axis=1, keepdims=True))
        probs_f = jnp.where(allowed, jnp.exp(scores - lse), 0.0)
        probs = probs_f.astype(jnp.bfloat16)
        value_term = lax.dot_general(
            probs, grad_head, (((0,), (0,)), ((), ())), preferred_element_type=jnp.float32
        )
        dprobs = lax.dot_general(
            grad_head, value_head, (((1,), (1,)), ((), ())), preferred_element_type=jnp.float32
        )
        delta = jnp.sum(
            grad_head.astype(jnp.float32) * output_head.astype(jnp.float32), axis=1, keepdims=True
        )
        dscores = (probs_f * (dprobs - delta)).astype(jnp.bfloat16)
        query_grad = (
            jnp.dot(dscores, key_head, preferred_element_type=jnp.float32) * score_scale
        ).astype(jnp.bfloat16)
        key_term = (
            lax.dot_general(
                dscores, query_head, (((0,), (0,)), ((), ())), preferred_element_type=jnp.float32
            )
            * score_scale
        )
        return (query_grad, key_term, value_term)

    query_grads, key_terms, value_terms = lax.map(
        one_head, (query_heads, grad_heads, output_heads, kv_ids)
    )
    grad_query = query_grads.transpose(1, 0, 2).reshape(quarter, feat_width)
    local_groups = max(1, heads_dev // group_size)

    def fold_local(terms):
        folded = terms.reshape(local_groups, heads_dev // local_groups, seq_len, HEAD_DIM).sum(axis=1)
        return folded.transpose(1, 0, 2).reshape(seq_len, local_groups * HEAD_DIM)

    def fold_remote(recv):
        spread = recv.shape[1] // (KV_HEADS * HEAD_DIM)
        folded = recv.reshape(recv.shape[0], KV_HEADS, spread, HEAD_DIM).sum(axis=2)
        return folded.reshape(recv.shape[0], KV_HEADS * HEAD_DIM)

    key_recv = lax.all_to_all(fold_local(key_terms), "ctx", split_axis=0, concat_axis=1, tiled=True)
    value_recv = lax.all_to_all(
        fold_local(value_terms), "ctx", split_axis=0, concat_axis=1, tiled=True
    )
    key_part = lax.psum_scatter(fold_remote(key_recv), "tsp", scatter_dimension=0, tiled=True)
    value_part = lax.psum_scatter(fold_remote(value_recv), "tsp", scatter_dimension=0, tiled=True)
    grad_keys = key_part.astype(jnp.bfloat16)[None]
    grad_values = value_part.astype(jnp.bfloat16)[None]
    return (grad_query[None], grad_keys, grad_values, grad_weight)


def solution(mesh):
    placed = (
        P("dp", "ctx", "tsp"),
        P("dp", None, "ctx"),
        P("ctx", "tsp"),
        P("dp", "tsp", "ctx"),
        P("dp", None, None),
        P("dp", None, None),
        P("dp", None),
        P("dp", None, None),
    )
    return jax.shard_map(
        per_device,
        mesh=mesh,
        in_specs=placed,
        out_specs=(
            P("dp", "tsp", "ctx"),
            P("dp", ("ctx", "tsp"), None),
            P("dp", ("ctx", "tsp"), None),
            P("ctx", "tsp"),
        ),
        check_vma=False,
    )
```

```python
import math

import jax
import jax.numpy as jnp
from jax import lax
from jax.sharding import PartitionSpec as P

HEADS = 32
KV_HEADS = 4
HEAD_DIM = 128
TILE = 128


def merge_group(tensor_in):
    row_count = tensor_in.shape[0]
    folded = tensor_in.reshape(row_count, KV_HEADS, HEADS // KV_HEADS, HEAD_DIM).sum(axis=2)
    return folded.reshape(row_count, KV_HEADS * HEAD_DIM)


def per_device(grad_out, attn_out, out_weight, query, keys, values, segment_ids, tile_live):
    score_scale = 1.0 / math.sqrt(HEAD_DIM)
    out_all = attn_out[0]
    seq_len = out_all.shape[0]
    feat_width = out_all.shape[1]
    dy_block = lax.all_gather(grad_out, "ctx", axis=1, tiled=True)[0]
    proj_rows = lax.dot_general(
        dy_block, out_weight, (((1,), (1,)), ((), ())), preferred_element_type=jnp.float32
    )
    grad_part = proj_rows
    weight_part = lax.dot_general(
        out_all, dy_block, (((0,), (0,)), ((), ())), preferred_element_type=jnp.float32
    )
    grad_part, weight_part = (grad_part, weight_part)
    weight_quarter = lax.psum_scatter(weight_part, "dp", scatter_dimension=0, tiled=True)
    grad_weight = lax.all_gather(
        weight_quarter.astype(jnp.bfloat16), "dp", axis=0, tiled=True
    ).astype(jnp.float32)
    out_grad = lax.psum_scatter(grad_part, "tsp", scatter_dimension=0, tiled=True).astype(
        jnp.bfloat16
    )
    quarter = out_grad.shape[0]
    row_start = lax.axis_index("tsp") * quarter
    heads_dev = feat_width // HEAD_DIM
    group_size = HEADS // KV_HEADS
    head_ids = lax.axis_index("ctx") * heads_dev + jnp.arange(heads_dev, dtype=jnp.int32)
    kv_ids = head_ids // group_size
    query_pos = row_start + jnp.arange(quarter, dtype=jnp.int32)
    key_pos = jnp.arange(seq_len, dtype=jnp.int32)
    tile_count = seq_len // TILE
    tile_rows = lax.dynamic_slice_in_dim(tile_live[0], row_start // TILE, quarter // TILE, 0)
    tile_mask = (
        jnp.broadcast_to(
            tile_rows[:, None, :, None], (quarter // TILE, TILE, tile_count, TILE)
        ).reshape(quarter, seq_len)
        == 1
    )
    same_tile = query_pos[:, None] // TILE == key_pos[None, :] // TILE
    segments = segment_ids[0]
    query_seg = lax.dynamic_slice_in_dim(segments, row_start, quarter, 0)
    same_doc = (segments[None, :] == query_seg[:, None]) | (segments[None, :] == 0)
    allowed = (tile_mask | same_tile) & same_doc & (key_pos[None, :] <= query_pos[:, None])

    query_heads = query[0].reshape(quarter, heads_dev, HEAD_DIM)
    grad_heads = out_grad.reshape(quarter, heads_dev, HEAD_DIM)
    output_heads = lax.dynamic_slice_in_dim(out_all, row_start, quarter, 0).reshape(
        quarter, heads_dev, HEAD_DIM
    )
    key_heads = jnp.take(keys[0].reshape(seq_len, KV_HEADS, HEAD_DIM), kv_ids, axis=1)
    value_heads = jnp.take(values[0].reshape(seq_len, KV_HEADS, HEAD_DIM), kv_ids, axis=1)
    scores = (
        jnp.einsum("qhd,khd->hqk", query_heads, key_heads, preferred_element_type=jnp.float32)
        * score_scale
    )
    scores = jnp.where(allowed[None], scores, -jnp.inf)
    row_max = jnp.max(scores, axis=2, keepdims=True)
    lse = row_max + jnp.log(jnp.sum(jnp.exp(scores - row_max), axis=2, keepdims=True))
    probs_f = jnp.where(allowed[None], jnp.exp(scores - lse), 0.0)
    probs = probs_f.astype(jnp.bfloat16)
    value_terms = jnp.einsum(
        "hqk,qhd->hkd", probs, grad_heads, preferred_element_type=jnp.float32
    )
    dprobs = jnp.einsum("qhd,khd->hqk", grad_heads, value_heads, preferred_element_type=jnp.float32)
    delta = jnp.sum(
        grad_heads.astype(jnp.float32) * output_heads.astype(jnp.float32), axis=2
    ).T[:, :, None]
    dscores = (probs_f * (dprobs - delta)).astype(jnp.bfloat16)
    grad_query = (
        jnp.einsum("hqk,khd->qhd", dscores, key_heads, preferred_element_type=jnp.float32)
        * score_scale
    ).astype(jnp.bfloat16).reshape(quarter, feat_width)
    key_terms = (
        jnp.einsum("hqk,qhd->hkd", dscores, query_heads, preferred_element_type=jnp.float32)
        * score_scale
    )
    local_groups = max(1, heads_dev // group_size)

    def fold_local(terms):
        folded = terms.reshape(local_groups, heads_dev // local_groups, seq_len, HEAD_DIM).sum(axis=1)
        return folded.transpose(1, 0, 2).reshape(seq_len, local_groups * HEAD_DIM)

    def fold_remote(recv):
        spread = recv.shape[1] // (KV_HEADS * HEAD_DIM)
        folded = recv.reshape(recv.shape[0], KV_HEADS, spread, HEAD_DIM).sum(axis=2)
        return folded.reshape(recv.shape[0], KV_HEADS * HEAD_DIM)

    key_recv = lax.all_to_all(fold_local(key_terms), "ctx", split_axis=0, concat_axis=1, tiled=True)
    value_recv = lax.all_to_all(
        fold_local(value_terms), "ctx", split_axis=0, concat_axis=1, tiled=True
    )
    key_part = lax.psum_scatter(fold_remote(key_recv), "tsp", scatter_dimension=0, tiled=True)
    value_part = lax.psum_scatter(fold_remote(value_recv), "tsp", scatter_dimension=0, tiled=True)
    grad_keys = key_part.astype(jnp.bfloat16)[None]
    grad_values = value_part.astype(jnp.bfloat16)[None]
    return (grad_query[None], grad_keys, grad_values, grad_weight)


def solution(mesh):
    placed = (
        P("dp", "ctx", "tsp"),
        P("dp", None, "ctx"),
        P("ctx", "tsp"),
        P("dp", "tsp", "ctx"),
        P("dp", None, None),
        P("dp", None, None),
        P("dp", None),
        P("dp", None, None),
    )
    return jax.shard_map(
        per_device,
        mesh=mesh,
        in_specs=placed,
        out_specs=(
            P("dp", "tsp", "ctx"),
            P("dp", ("ctx", "tsp"), None),
            P("dp", ("ctx", "tsp"), None),
            P("ctx", "tsp"),
        ),
        check_vma=False,
    )
```

```python
import math

import jax
import jax.numpy as jnp
from jax import lax
from jax.sharding import PartitionSpec as P

HEADS = 32
KV_HEADS = 4
HEAD_DIM = 128
TILE = 128


def merge_group(tensor_in):
    row_count = tensor_in.shape[0]
    folded = tensor_in.reshape(row_count, KV_HEADS, HEADS // KV_HEADS, HEAD_DIM).sum(axis=2)
    return folded.reshape(row_count, KV_HEADS * HEAD_DIM)


def per_device(grad_out, attn_out, out_weight, query, keys, values, segment_ids, tile_live):
    score_scale = 1.0 / math.sqrt(HEAD_DIM)
    out_all = attn_out[0]
    seq_len = out_all.shape[0]
    feat_width = out_all.shape[1]
    dy_block = lax.all_gather(grad_out, "ctx", axis=1, tiled=True)[0]
    proj_rows = lax.dot_general(
        dy_block, out_weight, (((1,), (1,)), ((), ())), preferred_element_type=jnp.float32
    )
    grad_part = proj_rows
    weight_part = lax.dot_general(
        out_all, dy_block, (((0,), (0,)), ((), ())), preferred_element_type=jnp.float32
    )
    grad_part, weight_part = (grad_part, weight_part)
    weight_quarter = lax.psum_scatter(
        weight_part.astype(jnp.bfloat16), "dp", scatter_dimension=0, tiled=True
    )
    grad_weight = lax.all_gather(weight_quarter, "dp", axis=0, tiled=True).astype(jnp.float32)
    out_grad = lax.psum_scatter(grad_part, "tsp", scatter_dimension=0, tiled=True).astype(
        jnp.bfloat16
    )
    quarter = out_grad.shape[0]
    row_start = lax.axis_index("tsp") * quarter
    heads_dev = feat_width // HEAD_DIM
    group_size = HEADS // KV_HEADS
    head_ids = lax.axis_index("ctx") * heads_dev + jnp.arange(heads_dev, dtype=jnp.int32)
    kv_ids = head_ids // group_size
    query_pos = row_start + jnp.arange(quarter, dtype=jnp.int32)
    key_pos = jnp.arange(seq_len, dtype=jnp.int32)
    tile_count = seq_len // TILE
    tile_rows = lax.dynamic_slice_in_dim(tile_live[0], row_start // TILE, quarter // TILE, 0)
    tile_mask = (
        jnp.broadcast_to(
            tile_rows[:, None, :, None], (quarter // TILE, TILE, tile_count, TILE)
        ).reshape(quarter, seq_len)
        == 1
    )
    same_tile = query_pos[:, None] // TILE == key_pos[None, :] // TILE
    segments = segment_ids[0]
    query_seg = lax.dynamic_slice_in_dim(segments, row_start, quarter, 0)
    same_doc = (segments[None, :] == query_seg[:, None]) | (segments[None, :] == 0)
    allowed = (tile_mask | same_tile) & same_doc & (key_pos[None, :] <= query_pos[:, None])

    query_heads = query[0].reshape(quarter, heads_dev, HEAD_DIM)
    grad_heads = out_grad.reshape(quarter, heads_dev, HEAD_DIM)
    output_heads = lax.dynamic_slice_in_dim(out_all, row_start, quarter, 0).reshape(
        quarter, heads_dev, HEAD_DIM
    )
    key_heads = jnp.take(keys[0].reshape(seq_len, KV_HEADS, HEAD_DIM), kv_ids, axis=1)
    value_heads = jnp.take(values[0].reshape(seq_len, KV_HEADS, HEAD_DIM), kv_ids, axis=1)
    scores = (
        jnp.einsum("qhd,khd->hqk", query_heads, key_heads, preferred_element_type=jnp.float32)
        * score_scale
    )
    scores = jnp.where(allowed[None], scores, -jnp.inf)
    row_max = jnp.max(scores, axis=2, keepdims=True)
    lse = row_max + jnp.log(jnp.sum(jnp.exp(scores - row_max), axis=2, keepdims=True))
    probs_f = jnp.where(allowed[None], jnp.exp(scores - lse), 0.0)
    probs = probs_f.astype(jnp.bfloat16)
    value_terms = jnp.einsum(
        "hqk,qhd->hkd", probs, grad_heads, preferred_element_type=jnp.float32
    )
    dprobs = jnp.einsum("qhd,khd->hqk", grad_heads, value_heads, preferred_element_type=jnp.float32)
    delta = jnp.sum(
        grad_heads.astype(jnp.float32) * output_heads.astype(jnp.float32), axis=2
    ).T[:, :, None]
    dscores = (probs_f * (dprobs - delta)).astype(jnp.bfloat16)
    grad_query = (
        jnp.einsum("hqk,khd->qhd", dscores, key_heads, preferred_element_type=jnp.float32)
        * score_scale
    ).astype(jnp.bfloat16).reshape(quarter, feat_width)
    key_terms = (
        jnp.einsum("hqk,qhd->hkd", dscores, query_heads, preferred_element_type=jnp.float32)
        * score_scale
    )
    local_groups = max(1, heads_dev // group_size)

    def fold_local(terms):
        folded = terms.reshape(local_groups, heads_dev // local_groups, seq_len, HEAD_DIM).sum(axis=1)
        return folded.transpose(1, 0, 2).reshape(seq_len, local_groups * HEAD_DIM)

    def fold_remote(recv):
        spread = recv.shape[1] // (KV_HEADS * HEAD_DIM)
        folded = recv.reshape(recv.shape[0], KV_HEADS, spread, HEAD_DIM).sum(axis=2)
        return folded.reshape(recv.shape[0], KV_HEADS * HEAD_DIM)

    key_recv = lax.all_to_all(fold_local(key_terms), "ctx", split_axis=0, concat_axis=1, tiled=True)
    value_recv = lax.all_to_all(
        fold_local(value_terms), "ctx", split_axis=0, concat_axis=1, tiled=True
    )
    key_part = lax.psum_scatter(fold_remote(key_recv), "tsp", scatter_dimension=0, tiled=True)
    value_part = lax.psum_scatter(fold_remote(value_recv), "tsp", scatter_dimension=0, tiled=True)
    grad_keys = key_part.astype(jnp.bfloat16)[None]
    grad_values = value_part.astype(jnp.bfloat16)[None]
    return (grad_query[None], grad_keys, grad_values, grad_weight)


def solution(mesh):
    placed = (
        P("dp", "ctx", "tsp"),
        P("dp", None, "ctx"),
        P("ctx", "tsp"),
        P("dp", "tsp", "ctx"),
        P("dp", None, None),
        P("dp", None, None),
        P("dp", None),
        P("dp", None, None),
    )
    return jax.shard_map(
        per_device,
        mesh=mesh,
        in_specs=placed,
        out_specs=(
            P("dp", "tsp", "ctx"),
            P("dp", ("ctx", "tsp"), None),
            P("dp", ("ctx", "tsp"), None),
            P("ctx", "tsp"),
        ),
        check_vma=False,
    )
```

```python
import math

import jax
import jax.numpy as jnp
from jax import lax
from jax.sharding import PartitionSpec as P

HEADS = 32
KV_HEADS = 4
HEAD_DIM = 128
TILE = 128


def merge_group(tensor_in):
    row_count = tensor_in.shape[0]
    folded = tensor_in.reshape(row_count, KV_HEADS, HEADS // KV_HEADS, HEAD_DIM).sum(axis=2)
    return folded.reshape(row_count, KV_HEADS * HEAD_DIM)


def per_device(grad_out, attn_out, out_weight, query, keys, values, segment_ids, tile_live):
    score_scale = 1.0 / math.sqrt(HEAD_DIM)
    out_all = attn_out[0]
    seq_len = out_all.shape[0]
    feat_width = out_all.shape[1]
    dy_local = grad_out[0]
    chunk_width = dy_local.shape[1] // 2
    proj_rows = None
    weight_cols = []
    for chunk_index in range(2):
        chunk_cols = slice(chunk_index * chunk_width, (chunk_index + 1) * chunk_width)
        dy_chunk = lax.all_gather(dy_local[:, chunk_cols], "ctx", axis=0, tiled=True)
        proj_chunk = lax.dot_general(
            dy_chunk, out_weight[:, chunk_cols], (((1,), (1,)), ((), ())),
            preferred_element_type=jnp.float32,
        )
        proj_rows = proj_chunk if proj_rows is None else proj_rows + proj_chunk
        weight_chunk = lax.dot_general(
            out_all, dy_chunk, (((0,), (0,)), ((), ())), preferred_element_type=jnp.float32
        )
        weight_quarter = lax.psum_scatter(
            weight_chunk.astype(jnp.bfloat16), "dp", scatter_dimension=0, tiled=True
        )
        weight_cols.append(lax.all_gather(weight_quarter, "dp", axis=0, tiled=True))
    grad_weight = jnp.concatenate(weight_cols, axis=1).astype(jnp.float32)
    grad_part = proj_rows
    out_grad = lax.psum_scatter(grad_part, "tsp", scatter_dimension=0, tiled=True).astype(
        jnp.bfloat16
    )
    quarter = out_grad.shape[0]
    row_start = lax.axis_index("tsp") * quarter
    heads_dev = feat_width // HEAD_DIM
    group_size = HEADS // KV_HEADS
    head_ids = lax.axis_index("ctx") * heads_dev + jnp.arange(heads_dev, dtype=jnp.int32)
    kv_ids = head_ids // group_size
    query_pos = row_start + jnp.arange(quarter, dtype=jnp.int32)
    key_pos = jnp.arange(seq_len, dtype=jnp.int32)
    tile_count = seq_len // TILE
    tile_rows = lax.dynamic_slice_in_dim(tile_live[0], row_start // TILE, quarter // TILE, 0)
    tile_mask = (
        jnp.broadcast_to(
            tile_rows[:, None, :, None], (quarter // TILE, TILE, tile_count, TILE)
        ).reshape(quarter, seq_len)
        == 1
    )
    same_tile = query_pos[:, None] // TILE == key_pos[None, :] // TILE
    segments = segment_ids[0]
    query_seg = lax.dynamic_slice_in_dim(segments, row_start, quarter, 0)
    same_doc = (segments[None, :] == query_seg[:, None]) | (segments[None, :] == 0)
    allowed = (tile_mask | same_tile) & same_doc & (key_pos[None, :] <= query_pos[:, None])

    query_heads = query[0].reshape(quarter, heads_dev, HEAD_DIM)
    grad_heads = out_grad.reshape(quarter, heads_dev, HEAD_DIM)
    output_heads = lax.dynamic_slice_in_dim(out_all, row_start, quarter, 0).reshape(
        quarter, heads_dev, HEAD_DIM
    )
    key_heads = jnp.take(keys[0].reshape(seq_len, KV_HEADS, HEAD_DIM), kv_ids, axis=1)
    value_heads = jnp.take(values[0].reshape(seq_len, KV_HEADS, HEAD_DIM), kv_ids, axis=1)
    scores = (
        jnp.einsum("qhd,khd->hqk", query_heads, key_heads, preferred_element_type=jnp.float32)
        * score_scale
    )
    scores = jnp.where(allowed[None], scores, -jnp.inf)
    row_max = jnp.max(scores, axis=2, keepdims=True)
    lse = row_max + jnp.log(jnp.sum(jnp.exp(scores - row_max), axis=2, keepdims=True))
    probs_f = jnp.where(allowed[None], jnp.exp(scores - lse), 0.0)
    probs = probs_f.astype(jnp.bfloat16)
    value_terms = jnp.einsum(
        "hqk,qhd->hkd", probs, grad_heads, preferred_element_type=jnp.float32
    )
    dprobs = jnp.einsum("qhd,khd->hqk", grad_heads, value_heads, preferred_element_type=jnp.float32)
    delta = jnp.sum(
        grad_heads.astype(jnp.float32) * output_heads.astype(jnp.float32), axis=2
    ).T[:, :, None]
    dscores = (probs_f * (dprobs - delta)).astype(jnp.bfloat16)
    grad_query = (
        jnp.einsum("hqk,khd->qhd", dscores, key_heads, preferred_element_type=jnp.float32)
        * score_scale
    ).astype(jnp.bfloat16).reshape(quarter, feat_width)
    key_terms = (
        jnp.einsum("hqk,qhd->hkd", dscores, query_heads, preferred_element_type=jnp.float32)
        * score_scale
    )
    local_groups = max(1, heads_dev // group_size)

    def fold_local(terms):
        folded = terms.reshape(local_groups, heads_dev // local_groups, seq_len, HEAD_DIM).sum(axis=1)
        return folded.transpose(1, 0, 2).reshape(seq_len, local_groups * HEAD_DIM)

    def fold_remote(recv):
        spread = recv.shape[1] // (KV_HEADS * HEAD_DIM)
        folded = recv.reshape(recv.shape[0], KV_HEADS, spread, HEAD_DIM).sum(axis=2)
        return folded.reshape(recv.shape[0], KV_HEADS * HEAD_DIM)

    key_recv = lax.all_to_all(fold_local(key_terms), "ctx", split_axis=0, concat_axis=1, tiled=True)
    value_recv = lax.all_to_all(
        fold_local(value_terms), "ctx", split_axis=0, concat_axis=1, tiled=True
    )
    key_part = lax.psum_scatter(fold_remote(key_recv), "tsp", scatter_dimension=0, tiled=True)
    value_part = lax.psum_scatter(fold_remote(value_recv), "tsp", scatter_dimension=0, tiled=True)
    grad_keys = key_part.astype(jnp.bfloat16)[None]
    grad_values = value_part.astype(jnp.bfloat16)[None]
    return (grad_query[None], grad_keys, grad_values, grad_weight)


def solution(mesh):
    placed = (
        P("dp", "ctx", "tsp"),
        P("dp", None, "ctx"),
        P("ctx", "tsp"),
        P("dp", "tsp", "ctx"),
        P("dp", None, None),
        P("dp", None, None),
        P("dp", None),
        P("dp", None, None),
    )
    return jax.shard_map(
        per_device,
        mesh=mesh,
        in_specs=placed,
        out_specs=(
            P("dp", "tsp", "ctx"),
            P("dp", ("ctx", "tsp"), None),
            P("dp", ("ctx", "tsp"), None),
            P("ctx", "tsp"),
        ),
        check_vma=False,
    )
```
